32 devices in a mesh: groups: 2 (over x), rows: 16 (over z, y, core).
Axes of the slice: x: 2, y: 2, z: 4, core: 2. Of those that a mesh axis runs over, the one named last changes fastest.
Arguments:
- queries: bfloat16 [64, 4096], P(('groups', 'rows')), parts along dimension 0, may hold values from -128 to 128
- new_keys: bfloat16 [64, 4096], P(('groups', 'rows')), parts along dimension 0, may hold values from -4 to 4
- new_values: bfloat16 [64, 4096], P(('groups', 'rows')), parts along dimension 0, may hold values from -5 to 5
- cache_keys: bfloat16 [64, 64, 4096], P(('groups', 'rows')), parts along dimension 0, may hold values from -4 to 4
- cache_values: bfloat16 [64, 64, 4096], P(('groups', 'rows')), parts along dimension 0, may hold values from -5 to 5
- cache_lengths: int32 [64], P(('groups', 'rows')), parts along dimension 0, may hold values from 1 to 64, as said below
- out_weight: bfloat16 [4096, 4096], P('rows'), may hold values from -0.09375 to 0.09375
- codes: int32 [64, 768], P(('groups', 'rows')), parts along dimension 0, may hold values from 0 to 1073741823
- tile_slot: int32 [64], P(('groups', 'rows')), parts along dimension 0, may hold values from -1 to 3, as said below
- code_weight: float32 [5, 512], replicated, may hold values from -2.5 to 2.5
- conv_one: bfloat16 [3, 3, 512, 512], replicated, may hold values from -0.09375 to 0.09375
- conv_two: bfloat16 [3, 3, 512, 512], replicated, may hold values from -0.09375 to 0.09375
Outputs:
- mixed: bfloat16 [64, 4096], P(('groups', 'rows')), parts along dimension 0
- decoded: bfloat16 [256, 48, 512], P(('groups', 'rows')), parts along dimension 0
The draws below stay inside these ranges and needn't reach their ends.
There are 2 independent parts, one for each index of `groups`. The reference program is written for one: setup_inputs(seed, part) draws one part's arguments, and reference() takes and returns one part's arrays. A program takes and returns all parts, laid end to end along the dimension named above; an argument that names none is the same for every part. Nothing has to cross between parts.
Inputs may be any that keep to these rules, and one draw needn't show every extreme that they name: `cache_lengths`: some row's length is exactly 64. `tile_slot`: each slot 0 to 3 belongs to exactly one row; all other rows hold -1.
All inputs are finite; a program needn't handle non-finite values.
Results may differ from the reference program's by a relative error of at most 0.0075.
Values may be sent and summed in bfloat16 or wider, within the bound.
A program may use at most 64 MiB of HBM per device.

```python
import math
import jax
import jax.numpy as jnp
from jax import lax

HEADS = 32
HEAD_DIM = 128
D = 4096
CACHE = 64
NROWS = 32
CHAN = 512
FSQ_DIMS = 5
IMG_W = 48
IMG_H = 32
WORDS = 768
SLOTS = 4


def attention_fields(key):
    base = jax.random.fold_in(key, 11)
    first_key, second_key, third_key = jax.random.split(base, 3)
    stored = jnp.clip(jax.random.normal(first_key, (NROWS, CACHE, D), jnp.float32), -4.0, 4.0)
    asking = jnp.clip(jax.random.normal(second_key, (NROWS, D), jnp.float32), -4.0, 4.0)
    fresh = jnp.clip(jax.random.normal(third_key, (NROWS, D), jnp.float32), -4.0, 4.0)
    return (stored, asking, fresh)


def draw_queries(key, part):
    return attention_fields(key)[1].astype(jnp.bfloat16)


def draw_new_keys(key, part):
    return attention_fields(key)[2].astype(jnp.bfloat16)


def draw_cache_keys(key, part):
    return attention_fields(key)[0].astype(jnp.bfloat16)


def draw_cache_lengths(key, part):
    first_key, second_key = jax.random.split(jax.random.fold_in(key, 23))
    lengths = jax.random.randint(first_key, (NROWS,), 1, CACHE + 1, jnp.int32)
    longest = jax.random.randint(second_key, (), 0, NROWS, jnp.int32)
    return lengths.at[longest].set(CACHE)


def draw_tile_slot(key, part):
    order = jax.random.permutation(jax.random.fold_in(key, 37), NROWS)
    chosen = order[:SLOTS]
    empty = jnp.full((NROWS,), -1, jnp.int32)
    return empty.at[chosen].set(jnp.arange(SLOTS, dtype=jnp.int32))


def set_ends(drawn, key, least, largest):
    dims = drawn.shape
    index_at = [jax.random.randint(jax.random.fold_in(key, axis), (), 0, dims[axis]) for axis in range(len(dims))]
    drawn = drawn.at[tuple(index_at)].set(least)
    longest = dims.index(max(dims))
    index_at[longest] = (index_at[longest] + 1) % dims[longest]
    return drawn.at[tuple(index_at)].set(largest)


def block_scale(stream_key, dims, cuts, low, top_value):
    gain, own = 1.0, jax.random.fold_in(stream_key, 6)
    for dim, parts in cuts:
        steps = jnp.exp(jax.random.uniform(jax.random.fold_in(own, dim), (parts,), jnp.float32, low / len(cuts), top_value / len(cuts)))
        gain = gain * jnp.repeat(steps, dims[dim] // parts).reshape([-1 if axis == dim else 1 for axis in range(len(dims))])
    return gain


def gaussian(stream_key, dims, deviation, limit, pieces=(), kind=jnp.bfloat16):
    values = jax.random.normal(stream_key, dims, jnp.float32) * deviation
    if len(pieces) > 0:
        values = block_scale(stream_key, dims, pieces, -0.22, 0.18) * values
    return jnp.clip(values, min=-limit, max=limit).astype(kind)


def setup_inputs(seed: int = 0, part: int = 0) -> dict:
    splits = jax.random.split(jax.random.key(seed), 13)
    own_keys = jax.random.split(jax.random.fold_in(splits[12], part), 13)
    return {
        "queries": draw_queries(jax.random.fold_in(jax.random.fold_in(splits[12], part), 71), part),
        "new_keys": draw_new_keys(jax.random.fold_in(jax.random.fold_in(splits[12], part), 71), part),
        "new_values": gaussian(own_keys[2], (NROWS, D), 1.0, 5.0, ((0, 16),)),
        "cache_keys": draw_cache_keys(jax.random.fold_in(jax.random.fold_in(splits[12], part), 71), part),
        "cache_values": gaussian(own_keys[4], (NROWS, CACHE, D), 1.0, 5.0, ((0, 16),)),
        "cache_lengths": draw_cache_lengths(jax.random.fold_in(jax.random.fold_in(splits[12], part), 71), part),
        "out_weight": gaussian(splits[6], (D, D), D ** -0.5, 0.09375, ((0, 16),)),
        "codes": set_ends(jax.random.randint(own_keys[7], (NROWS, WORDS), 0, 1073741824), jax.random.fold_in(own_keys[7], 1), 0, 1073741823).astype(jnp.int32),
        "tile_slot": draw_tile_slot(jax.random.fold_in(jax.random.fold_in(splits[12], part), 71), part),
        "code_weight": gaussian(splits[9], (FSQ_DIMS, CHAN), FSQ_DIMS ** -0.5, 2.5, (), jnp.float32),
        "conv_one": gaussian(splits[10], (3, 3, CHAN, CHAN), (9 * CHAN) ** -0.5, 0.09375),
        "conv_two": gaussian(splits[11], (3, 3, CHAN, CHAN), (9 * CHAN) ** -0.5, 0.09375),
    }


def convolve(padded, weights):
    out_h = padded.shape[0] - 2
    out_w = padded.shape[1] - 2
    channels = padded.shape[2]
    summed = jnp.zeros((out_h * out_w, weights.shape[3]), jnp.float32)
    for row_step in range(3):
        for col_step in range(3):
            window = padded[row_step:row_step + out_h, col_step:col_step + out_w].reshape(out_h * out_w, channels)
            summed = summed + jnp.dot(window, weights[row_step, col_step], preferred_element_type=jnp.float32)
    return summed.reshape(out_h, out_w, weights.shape[3])

def unpack(words, code_weight):
    lower = words % 32768
    upper = words // 32768
    position_codes = jnp.stack([lower, upper], 1).reshape(-1)
    levels = jnp.stack([position_codes // 8 ** level % 8 for level in range(FSQ_DIMS)], 1)
    values = (2 * levels - 7).astype(jnp.float32) * 0.125
    return jnp.dot(values, code_weight, precision=lax.Precision.HIGHEST, preferred_element_type=jnp.float32)

def attend(queries, new_keys, new_values, cache_keys, cache_values, cache_lengths):
    count = queries.shape[0]
    factor = 1.0 / math.sqrt(HEAD_DIM)
    query_heads = queries.astype(jnp.float32).reshape(count, HEADS, HEAD_DIM)
    key_heads = cache_keys.astype(jnp.float32).reshape(count, -1, HEADS, HEAD_DIM)
    value_heads = cache_values.astype(jnp.float32).reshape(count, -1, HEADS, HEAD_DIM)
    scores = jnp.einsum('rhd,rlhd->rhl', query_heads, key_heads) * factor
    own_score = lax.optimization_barrier(jnp.sum(query_heads * new_keys.astype(jnp.float32).reshape(count, HEADS, HEAD_DIM), -1)) * factor
    live = jnp.arange(key_heads.shape[1], dtype=jnp.int32)[None, None, :] < cache_lengths[:, None, None]
    scores = jnp.where(live, scores, jnp.float32(-1e+30))
    highest = jnp.maximum(lax.optimization_barrier(jnp.max(scores, -1)), own_score)
    cache_exp = jnp.where(live, jnp.exp(scores - highest[..., None]), jnp.float32(0.0))
    own_exp = jnp.exp(own_score - highest)
    denom = lax.optimization_barrier(jnp.sum(cache_exp, -1)) + own_exp
    cache_weight = (cache_exp / denom[..., None]).astype(jnp.bfloat16)
    own_weight = (own_exp / denom).astype(jnp.bfloat16)
    attended = jnp.einsum('rhl,rlhd->rhd', cache_weight.astype(jnp.float32), value_heads)
    attended = attended + own_weight.astype(jnp.float32)[..., None] * new_values.astype(jnp.float32).reshape(count, HEADS, HEAD_DIM)
    return attended.reshape(count, HEADS * HEAD_DIM).astype(jnp.bfloat16)

def reference(queries, new_keys, new_values, cache_keys, cache_values, cache_lengths, out_weight, codes, tile_slot, code_weight, conv_one, conv_two):
    attended = attend(queries, new_keys, new_values, cache_keys, cache_values, cache_lengths)
    mixed = jnp.dot(attended, out_weight, preferred_element_type=jnp.float32).astype(jnp.bfloat16)

    def decode_one(slot):
        chosen = lax.optimization_barrier(jnp.sum(jnp.where((tile_slot == slot)[:, None], codes, 0), 0)).astype(jnp.int32)
        latent = unpack(chosen, code_weight).reshape(IMG_H, IMG_W, -1).astype(jnp.bfloat16)
        padded = jnp.pad(latent, ((1, 1), (1, 1), (0, 0)))
        hidden = convolve(padded, conv_one)
        activated = jax.nn.silu(hidden).astype(jnp.bfloat16)
        padded_two = jnp.pad(activated, ((1, 1), (1, 1), (0, 0)))
        return convolve(padded_two, conv_two).astype(jnp.bfloat16)
    images = lax.map(decode_one, jnp.arange(SLOTS, dtype=jnp.int32))
    stacked = images.reshape(SLOTS * IMG_H, IMG_W, images.shape[3])
    decoded = jnp.roll(stacked, -(IMG_H // 2), axis=0)
    return (mixed, decoded)
```

```python
import math

import jax
import jax.numpy as jnp
from jax import lax
from jax.sharding import PartitionSpec as P

HEADS = 32
HEAD_DIM = 128
FSQ_DIMS = 5
IMG_SPLIT = 4
TILE_H = 8
IMG_W = 48


def convolve(padded, weights):
    out_h = padded.shape[0] - 2
    out_w = padded.shape[1] - 2
    channels = padded.shape[2]
    summed = jnp.zeros((out_h * out_w, weights.shape[3]), jnp.float32)
    for row_step in range(3):
        for col_step in range(3):
            window = padded[row_step : row_step + out_h, col_step : col_step + out_w].reshape(
                out_h * out_w, channels
            )
            summed = summed + jnp.dot(
                window, weights[row_step, col_step], preferred_element_type=jnp.float32
            )
    return summed.reshape(out_h, out_w, weights.shape[3])


def unpack(words, code_weight):
    lower = words % 32768
    upper = words // 32768
    position_codes = jnp.stack([lower, upper], 1).reshape(-1)
    levels = jnp.stack([position_codes // 8**level % 8 for level in range(FSQ_DIMS)], 1)
    values = (2 * levels - 7).astype(jnp.float32) * 0.125
    return jnp.dot(
        values, code_weight, precision=lax.Precision.HIGHEST, preferred_element_type=jnp.float32
    )


def attend(queries, new_keys, new_values, cache_keys, cache_values, cache_lengths):
    count = queries.shape[0]
    factor = 1.0 / math.sqrt(HEAD_DIM)
    query_heads = queries.reshape(count, HEADS, HEAD_DIM)
    key_heads = cache_keys.reshape(count, -1, HEADS, HEAD_DIM)
    value_heads = cache_values.reshape(count, -1, HEADS, HEAD_DIM)
    scores = (
        jnp.einsum("rhd,rlhd->rhl", query_heads, key_heads, preferred_element_type=jnp.float32)
        * factor
    )
    own_score = (
        jnp.sum(
            query_heads.astype(jnp.float32)
            * new_keys.astype(jnp.float32).reshape(count, HEADS, HEAD_DIM),
            -1,
        )
        * factor
    )
    live = (
        jnp.arange(key_heads.shape[1], dtype=jnp.int32)[None, None, :]
        < cache_lengths[:, None, None]
    )
    scores = jnp.where(live, scores, jnp.float32(-1e30))
    highest = jnp.maximum(jnp.max(scores, -1), own_score)
    cache_exp = jnp.where(live, jnp.exp(scores - highest[..., None]), jnp.float32(0.0))
    own_exp = jnp.exp(own_score - highest)
    denom = jnp.sum(cache_exp, -1) + own_exp
    cache_weight = (cache_exp / denom[..., None]).astype(jnp.bfloat16)
    own_weight = (own_exp / denom).astype(jnp.bfloat16)
    attended = jnp.einsum(
        "rhl,rlhd->rhd", cache_weight, value_heads, preferred_element_type=jnp.float32
    )
    attended = attended + own_weight.astype(jnp.float32)[..., None] * new_values.astype(
        jnp.float32
    ).reshape(count, HEADS, HEAD_DIM)
    return attended.reshape(count, HEADS * HEAD_DIM).astype(jnp.bfloat16)


def clear_edges(field, depth, section):
    height = field.shape[0]
    line = jnp.arange(height, dtype=jnp.int32)[:, None, None]
    cleared = (line < depth) & (section == 0) | (line >= height - depth) & (
        section == IMG_SPLIT - 1
    )
    return jnp.where(cleared, jnp.zeros((), field.dtype), field)


def widen_columns(field):
    return jnp.pad(field, ((0, 0), (1, 1), (0, 0)))


def on_device(
    queries,
    new_keys,
    new_values,
    cache_keys,
    cache_values,
    cache_lengths,
    out_weight,
    codes,
    tile_slot,
    code_weight,
    conv_one,
    conv_two,
):
    attended = attend(queries, new_keys, new_values, cache_keys, cache_values, cache_lengths)
    feature_rows = lax.all_to_all(attended, "rows", split_axis=1, concat_axis=0, tiled=True)
    own_count = attended.shape[0]
    partial_value = jnp.dot(feature_rows, out_weight, preferred_element_type=jnp.float32)
    shares = lax.all_to_all(
        partial_value.astype(jnp.bfloat16), "rows", split_axis=0, concat_axis=0, tiled=True
    )
    mixed = jnp.sum(
        shares.reshape(-1, own_count, shares.shape[1]).astype(jnp.float32), 0
    ).astype(jnp.bfloat16)
    tiles = lax.axis_size("rows")
    place = lax.axis_index("rows")
    tile_number = (place + IMG_SPLIT // 2) % tiles
    section = tile_number % IMG_SPLIT
    tile_words = TILE_H * IMG_W // 2
    rim_words = 2 * IMG_W // 2
    wide = jnp.pad(codes, ((0, 0), (rim_words, rim_words)))
    sections = jnp.stack(
        [wide[:, i * tile_words : (i + 1) * tile_words + 2 * rim_words] for i in range(IMG_SPLIT)], 1
    )
    destined = (jnp.arange(tiles, dtype=jnp.int32) + IMG_SPLIT // 2) % tiles
    target_slot = destined // IMG_SPLIT
    target_section = destined % IMG_SPLIT
    spread = jnp.take(sections, target_section, axis=1)
    matches = tile_slot[:, None] == target_slot[None, :]
    outgoing = jnp.sum(jnp.where(matches[:, :, None], spread, 0), 0)
    incoming = lax.all_to_all(outgoing, "rows", split_axis=0, concat_axis=0, tiled=True)
    chosen = jnp.sum(incoming, 0)
    latent = unpack(chosen, code_weight).reshape(TILE_H + 4, IMG_W, -1).astype(jnp.bfloat16)
    hidden = convolve(widen_columns(clear_edges(latent, 2, section)), conv_one)
    activated = jax.nn.silu(hidden).astype(jnp.bfloat16)
    decoded = convolve(widen_columns(clear_edges(activated, 1, section)), conv_two).astype(
        jnp.bfloat16
    )
    return (mixed, decoded)


def solution(mesh):
    in_specs = (
        P(("groups", "rows"), None),
        P(("groups", "rows"), None),
        P(("groups", "rows"), None),
        P(("groups", "rows"), None, None),
        P(("groups", "rows"), None, None),
        P(("groups", "rows")),
        P("rows", None),
        P(("groups", "rows"), None),
        P(("groups", "rows")),
        P(),
        P(),
        P(),
    )
    out_specs = (P(("groups", "rows"), None), P(("groups", "rows"), None, None))
    return jax.shard_map(
        on_device, mesh=mesh, in_specs=in_specs, out_specs=out_specs, check_vma=False
    )
```

```python
import functools
import math

import jax
import jax.numpy as jnp
from jax import lax
from jax.experimental import pallas as pl
from jax.experimental.pallas import tpu as pltpu
from jax.sharding import PartitionSpec as P

HEAD_DIM = 128
FSQ_DIMS = 5
IMG_H = 32
IMG_W = 48
IMG_SPLIT = 4
LANES = 128
PAD = 8
BF16 = jnp.bfloat16
F32 = jnp.float32
MESH = pl.DeviceIdType.MESH


def dot(a, b):
    return jnp.dot(a, b, preferred_element_type=F32)


def dot_nt(a, b):
    return lax.dot_general(a, b, (((1,), (1,)), ((), ())), preferred_element_type=F32)


def kernel(
    n,
    tile_h,
    lengths,
    tile_slot,
    queries,
    new_keys,
    new_values,
    codes,
    code_weight,
    cache_keys_hbm,
    cache_values_hbm,
    out_weight_hbm,
    conv_one_hbm,
    conv_two_hbm,
    mixed,
    decoded_hbm,
    cache_keys,
    cache_values,
    out_weight,
    conv_one,
    conv_two,
    slot_codes,
    codes_in,
    att_out,
    att_in,
    features,
    partial_rows,
    part_out,
    part_in,
    field,
    columns,
    shifted,
    decoded,
    local_sem,
    out_sem,
    code_send,
    code_recv,
    att_send,
    att_recv,
    part_send,
    part_recv,
):
    me = lax.axis_index("rows")
    own = queries.shape[0]
    width = queries.shape[1]
    heads = width // HEAD_DIM
    cache = cache_keys.shape[1]
    channels = code_weight.shape[1]
    sections = IMG_H // tile_h
    share = width // n
    block = att_out.shape[2]
    words = codes.shape[1]

    loads = [
        pltpu.make_async_copy(source, target, local_sem.at[i])
        for i, (source, target) in enumerate(
            (
                (cache_keys_hbm, cache_keys),
                (cache_values_hbm, cache_values),
                (conv_one_hbm, conv_one),
                (out_weight_hbm, out_weight),
                (conv_two_hbm, conv_two),
            )
        )
    ]
    for load in loads:
        load.start()

    barrier = pltpu.get_barrier_semaphore()

    @pl.loop(1, n)
    def _(k):
        pl.semaphore_signal(
            barrier, inc=1, device_id={"rows": lax.rem(me + k, n)}, device_id_type=MESH
        )

    for slot in range(n // sections):
        picked = jnp.zeros((1, words), jnp.int32)
        for r in range(own):
            picked = picked + jnp.where(tile_slot[r] == slot, codes[r : r + 1, :], 0)
        slot_codes[slot] = picked

    pl.semaphore_wait(barrier, n - 1)

    def slot_of(device):
        return lax.rem(device + sections // 2, n) // sections

    def code_copy(k):
        target = lax.rem(me + k, n)
        return pltpu.make_async_remote_copy(
            src_ref=slot_codes.at[slot_of(target)],
            dst_ref=codes_in.at[me],
            send_sem=code_send.at[k],
            recv_sem=code_recv.at[k],
            device_id={"rows": target},
            device_id_type=MESH,
        )

    def att_copy(k):
        target = lax.rem(me + k, n)
        return pltpu.make_async_remote_copy(
            src_ref=att_out.at[target],
            dst_ref=att_in.at[me],
            send_sem=att_send.at[k],
            recv_sem=att_recv.at[k],
            device_id={"rows": target},
            device_id_type=MESH,
        )

    def part_copy(k):
        target = lax.rem(me + k, n)
        return pltpu.make_async_remote_copy(
            src_ref=part_out.at[target],
            dst_ref=part_in.at[me],
            send_sem=part_send.at[k],
            recv_sem=part_recv.at[k],
            device_id={"rows": target},
            device_id_type=MESH,
        )

    @pl.loop(1, n)
    def _(k):
        code_copy(k).start()

    codes_in[me] = slot_codes[slot_of(me)]

    head_mask = (
        lax.broadcasted_iota(jnp.int32, (heads, width), 1) // HEAD_DIM
        == lax.broadcasted_iota(jnp.int32, (heads, width), 0)
    )
    factor = 1.0 / math.sqrt(HEAD_DIM)
    asking = queries[...].astype(F32)
    fresh_keys = new_keys[...].astype(F32)
    fresh_values = new_values[...].astype(F32)
    loads[0].wait()
    weights = []
    for r in range(own):
        spread = jnp.where(head_mask, asking[r : r + 1, :], 0.0)
        scores = dot_nt(spread.astype(BF16), cache_keys[r]) * factor
        own_score = jnp.sum(spread * fresh_keys[r : r + 1, :], axis=1, keepdims=True) * factor
        live = lax.broadcasted_iota(jnp.int32, (heads, cache), 1) < lengths[r]
        scores = jnp.where(live, scores, -1e30)
        highest = jnp.maximum(jnp.max(scores, axis=1, keepdims=True), own_score)
        cache_exp = jnp.where(live, jnp.exp(scores - highest), 0.0)
        own_exp = jnp.exp(own_score - highest)
        denom = jnp.sum(cache_exp, axis=1, keepdims=True) + own_exp
        weights.append(((cache_exp / denom).astype(BF16), (own_exp / denom).astype(BF16).astype(F32)))
    loads[1].wait()
    rows = []
    for r in range(own):
        cache_weight, own_weight = weights[r]
        full = dot(cache_weight, cache_values[r]) + own_weight * fresh_values[r : r + 1, :]
        rows.append(jnp.sum(jnp.where(head_mask, full, 0.0), axis=0, keepdims=True))
    attended = jnp.concatenate(rows, axis=0).astype(BF16).astype(F32)
    for d in range(n):
        start = d * share // LANES * LANES
        att_out[d] = attended[:, start : start + block]

    @pl.loop(1, n)
    def _(k):
        att_copy(k).start()

    att_in[me] = att_out[me]

    tile = lax.rem(me + sections // 2, n)
    section = lax.rem(tile, sections)
    tile_words = tile_h * IMG_W // 2
    span = (tile_h + 4) * IMG_W

    @pl.loop(1, n)
    def _(k):
        code_copy(k).wait()

    chosen = codes_in[0]
    for i in range(1, n):
        chosen = chosen + codes_in[i]
    turned = pltpu.roll(
        jnp.broadcast_to(chosen, (8, words)),
        lax.rem(words + IMG_W - section * tile_words, words),
        axis=1,
    )
    strip_words = -(-(span // 2) // LANES) * LANES
    strip = turned[0:1, 0:strip_words]
    level = lax.broadcasted_iota(jnp.int32, (16, strip_words), 0)
    level = jnp.where(level >= 2 * FSQ_DIMS, level - 2 * FSQ_DIMS, level)
    level = jnp.where(level >= FSQ_DIMS, level - FSQ_DIMS, level)
    strip = jnp.broadcast_to(strip, (16, strip_words))

    def values_of(position_codes):
        levels = jnp.right_shift(position_codes, 3 * level) & 7
        return ((2 * levels - 7).astype(F32) * 0.125).astype(BF16)

    low = values_of(strip & 32767)
    high = values_of(jnp.right_shift(strip, 15))
    place = lax.broadcasted_iota(jnp.int32, (span, strip_words), 0)
    word = lax.broadcasted_iota(jnp.int32, (span, strip_words), 1)
    gap = place - 2 * word
    even = jnp.where(gap == 0, 1.0, 0.0).astype(BF16)
    odd = jnp.where(gap == 1, 1.0, 0.0).astype(BF16)
    field[0:PAD, :] = jnp.zeros((PAD, 16), F32)
    field[PAD + span :, :] = jnp.zeros((PAD, 16), F32)
    field[PAD : PAD + span, :] = dot_nt(even, low) + dot_nt(odd, high)

    whole = code_weight[...]
    top = whole.astype(BF16)
    rest = whole - top.astype(F32)
    middle = rest.astype(BF16)
    bottom = rest - middle.astype(F32)
    thirds = jnp.concatenate(
        [top.astype(F32), middle.astype(F32), bottom, jnp.zeros((1, channels), F32)], axis=0
    ).astype(BF16)

    def kept(count, rim):
        position = lax.broadcasted_iota(jnp.int32, (count, 1), 0)
        inside = jnp.logical_not(
            ((position < rim * IMG_W) & (section == 0))
            | ((position >= count - rim * IMG_W) & (section == sections - 1))
        )
        column = lax.rem(position, IMG_W)
        return inside, (column != 0, None, column != IMG_W - 1)

    inside, edges = kept(span, 2)
    for i in range(3):
        piece = field[PAD + i - 1 : PAD + i - 1 + span, :]
        mask = inside if edges[i] is None else inside & edges[i]
        piece = jnp.where(mask, piece, 0.0).astype(BF16)
        shifted[:, i * channels : (i + 1) * channels] = dot(piece, thirds).astype(BF16)

    mid_span = (tile_h + 2) * IMG_W
    loads[2].wait()
    hidden = dot(shifted[0:mid_span, :], conv_one[0])
    for tap in range(1, 3):
        hidden = hidden + dot(shifted[tap * IMG_W : tap * IMG_W + mid_span, :], conv_one[tap])
    inside, edges = kept(mid_span, 1)
    activated = jnp.where(inside, jax.nn.silu(hidden), 0.0)
    columns[0:PAD, :] = jnp.zeros((PAD, channels), F32)
    columns[PAD + mid_span :, :] = jnp.zeros((PAD, channels), F32)
    columns[PAD : PAD + mid_span, :] = activated

    @pl.loop(1, n)
    def _(k):
        att_copy(k).wait()

    for i in range(n):
        features[own * i : own * (i + 1), :] = att_in[i]
    rows_in = features[...].astype(BF16)
    loads[3].wait()
    pieces = part_out.shape[1] // own
    piece_width = width // pieces
    for c in range(pieces):
        piece = dot(rows_in, out_weight[:, c * piece_width : (c + 1) * piece_width])
        for j in range(piece_width // LANES):
            partial_rows[j, pl.ds(c, own * n, stride=pieces), :] = piece[
                :, j * LANES : (j + 1) * LANES
            ]
    for i in range(n):
        for j in range(piece_width // LANES):
            part_out[i, :, j * LANES : (j + 1) * LANES] = partial_rows[
                j, own * pieces * i : own * pieces * (i + 1), :
            ].astype(BF16)

    @pl.loop(1, n)
    def _(k):
        part_copy(k).start()

    part_in[me] = part_out[me]

    for i in range(3):
        piece = columns[PAD + i - 1 : PAD + i - 1 + mid_span, :]
        if edges[i] is not None:
            piece = jnp.where(edges[i], piece, 0.0)
        shifted[0:mid_span, i * channels : (i + 1) * channels] = piece.astype(BF16)
    out_span = tile_h * IMG_W
    loads[4].wait()
    final = dot(shifted[0:out_span, :], conv_two[0])
    for tap in range(1, 3):
        final = final + dot(shifted[tap * IMG_W : tap * IMG_W + out_span, :], conv_two[tap])
    decoded[...] = final.astype(BF16)
    store = pltpu.make_async_copy(decoded, decoded_hbm, out_sem)
    store.start()

    @pl.loop(1, n)
    def _(k):
        part_copy(k).wait()

    total = part_in[0].astype(F32)
    for i in range(1, n):
        total = total + part_in[i].astype(F32)
    mixed[...] = total.astype(BF16)
    store.wait()


def on_device(
    n,
    queries,
    new_keys,
    new_values,
    cache_keys,
    cache_values,
    cache_lengths,
    out_weight,
    codes,
    tile_slot,
    code_weight,
    conv_one,
    conv_two,
):
    own, width = queries.shape
    channels = code_weight.shape[1]
    sections = IMG_SPLIT
    tile_h = IMG_H // sections
    share = out_weight.shape[0]
    block = max(share, LANES)
    if share < block:
        parts = block // share
        slot = lax.rem(lax.axis_index("rows"), parts)
        which = jnp.arange(parts, dtype=jnp.int32)[:, None, None] == slot
        out_weight = jnp.where(which, out_weight[None], jnp.zeros((), BF16)).reshape(block, width)
    taps = conv_one.shape[1] * channels
    conv_one = conv_one.reshape(3, taps, channels)
    conv_two = conv_two.reshape(3, taps, channels)
    pieces = 16 // own
    span = (tile_h + 4) * IMG_W
    mid_span = (tile_h + 2) * IMG_W
    out_span = tile_h * IMG_W
    vmem = pl.BlockSpec(memory_space=pltpu.VMEM)
    smem = pl.BlockSpec(memory_space=pltpu.SMEM)
    hbm = pl.BlockSpec(memory_space=pl.ANY)
    dma = pltpu.SemaphoreType.DMA
    mixed, decoded = pl.pallas_call(
        functools.partial(kernel, n, tile_h),
        out_shape=(
            jax.ShapeDtypeStruct((own * pieces, width // pieces), BF16),
            jax.ShapeDtypeStruct((out_span, channels), BF16),
        ),
        in_specs=[smem, smem, vmem, vmem, vmem, vmem, vmem, hbm, hbm, hbm, hbm, hbm],
        out_specs=(vmem, hbm),
        scratch_shapes=[
            pltpu.VMEM(cache_keys.shape, BF16),
            pltpu.VMEM(cache_values.shape, BF16),
            pltpu.VMEM(out_weight.shape, BF16),
            pltpu.VMEM(conv_one.shape, BF16),
            pltpu.VMEM(conv_two.shape, BF16),
            pltpu.VMEM((n // sections, 1, codes.shape[1]), jnp.int32),
            pltpu.VMEM((n, 1, codes.shape[1]), jnp.int32),
            pltpu.VMEM((n, own, block), F32),
            pltpu.VMEM((n, own, block), F32),
            pltpu.VMEM((n * own, block), F32),
            pltpu.VMEM((width // pieces // LANES, n * own * pieces, LANES), F32),
            pltpu.VMEM((n, own * pieces, width // pieces), BF16),
            pltpu.VMEM((n, own * pieces, width // pieces), BF16),
            pltpu.VMEM((span + 2 * PAD, 16), F32),
            pltpu.VMEM((mid_span + 2 * PAD, channels), F32),
            pltpu.VMEM((span, taps), BF16),
            pltpu.VMEM((out_span, channels), BF16),
            dma((5,)),
            dma(()),
            dma((n,)),
            dma((n,)),
            dma((n,)),
            dma((n,)),
            dma((n,)),
            dma((n,)),
        ],
        compiler_params=pltpu.CompilerParams(
            collective_id=0, has_side_effects=True, vmem_limit_bytes=60 * 1024 * 1024
        ),
        name="decode_step",
    )(
        cache_lengths,
        tile_slot,
        queries,
        new_keys,
        new_values,
        codes,
        code_weight,
        cache_keys,
        cache_values,
        out_weight,
        conv_one,
        conv_two,
    )
    return mixed.reshape(own, width), decoded.reshape(tile_h, IMG_W, channels)


def solution(mesh):
    both = ("groups", "rows")
    in_specs = (
        P(both, None),
        P(both, None),
        P(both, None),
        P(both, None, None),
        P(both, None, None),
        P(both),
        P("rows", None),
        P(both, None),
        P(both),
        P(),
        P(),
        P(),
    )
    out_specs = (P(both, None), P(both, None, None))
    return jax.shard_map(
        functools.partial(on_device, mesh.shape["rows"]),
        mesh=mesh,
        in_specs=in_specs,
        out_specs=out_specs,
        check_vma=False,
    )
```

```python
import functools
import math

import jax
import jax.numpy as jnp
from jax import lax
from jax.experimental import pallas as pl
from jax.experimental.pallas import tpu as pltpu
from jax.sharding import PartitionSpec as P

HEAD_DIM = 128
FSQ_DIMS = 5
IMG_H = 32
IMG_W = 48
IMG_SPLIT = 4
LANES = 128
PAD = 8
BF16 = jnp.bfloat16
F32 = jnp.float32
MESH = pl.DeviceIdType.MESH


def dot(a, b):
    return jnp.dot(a, b, preferred_element_type=F32)


def dot_nt(a, b):
    return lax.dot_general(a, b, (((1,), (1,)), ((), ())), preferred_element_type=F32)


def kernel(
    n,
    tile_h,
    lengths_hbm,
    tile_slot_hbm,
    queries_hbm,
    new_keys_hbm,
    new_values_hbm,
    codes_hbm,
    code_weight_hbm,
    cache_keys_hbm,
    cache_values_hbm,
    out_weight_hbm,
    conv_one_hbm,
    conv_two_hbm,
    mixed,
    decoded,
    lengths,
    tile_slot,
    queries,
    new_keys,
    new_values,
    codes,
    code_weight,
    cache_keys,
    cache_values,
    out_weight,
    conv_one,
    conv_two,
    slot_codes,
    codes_in,
    att_out,
    att_in,
    features,
    partial_rows,
    part_out,
    part_in,
    field,
    columns,
    shifted,
    local_sem,
    code_send,
    code_recv,
    att_send,
    att_recv,
    part_send,
    part_recv,
):
    me = lax.axis_index("rows")
    own = queries.shape[0]
    width = queries.shape[1]
    heads = width // HEAD_DIM
    cache = cache_keys.shape[1]
    channels = code_weight.shape[1]
    sections = IMG_H // tile_h
    share = width // n
    block = att_out.shape[2]
    words = codes.shape[1]

    barrier = pltpu.get_barrier_semaphore()

    @pl.loop(1, n)
    def _(k):
        pl.semaphore_signal(
            barrier, inc=1, device_id={"rows": lax.rem(me + k, n)}, device_id_type=MESH
        )

    loads = [
        pltpu.make_async_copy(source, target, local_sem.at[i])
        for i, (source, target) in enumerate(
            (
                (queries_hbm, queries),
                (new_keys_hbm, new_keys),
                (new_values_hbm, new_values),
                (lengths_hbm, lengths),
                (cache_keys_hbm, cache_keys),
                (cache_values_hbm, cache_values),
                (codes_hbm, codes),
                (tile_slot_hbm, tile_slot),
                (code_weight_hbm, code_weight),
                (out_weight_hbm, out_weight),
                (conv_one_hbm, conv_one),
                (conv_two_hbm, conv_two),
            )
        )
    ]
    for load in loads:
        load.start()

    def slot_of(device):
        return lax.rem(device + sections // 2, n) // sections

    def code_copy(k):
        target = lax.rem(me + k, n)
        return pltpu.make_async_remote_copy(
            src_ref=slot_codes.at[slot_of(target)],
            dst_ref=codes_in.at[me],
            send_sem=code_send.at[k],
            recv_sem=code_recv.at[k],
            device_id={"rows": target},
            device_id_type=MESH,
        )

    def att_copy(k):
        target = lax.rem(me + k, n)
        return pltpu.make_async_remote_copy(
            src_ref=att_out.at[target],
            dst_ref=att_in.at[me],
            send_sem=att_send.at[k],
            recv_sem=att_recv.at[k],
            device_id={"rows": target},
            device_id_type=MESH,
        )

    def part_copy(k):
        target = lax.rem(me + k, n)
        return pltpu.make_async_remote_copy(
            src_ref=part_out.at[target],
            dst_ref=part_in.at[me],
            send_sem=part_send.at[k],
            recv_sem=part_recv.at[k],
            device_id={"rows": target},
            device_id_type=MESH,
        )

    head_mask = (
        lax.broadcasted_iota(jnp.int32, (heads, width), 1) // HEAD_DIM
        == lax.broadcasted_iota(jnp.int32, (heads, width), 0)
    )
    factor = 1.0 / math.sqrt(HEAD_DIM)
    loads[0].wait()
    loads[1].wait()
    loads[2].wait()
    loads[3].wait()
    asking = queries[...].astype(F32)
    fresh_keys = new_keys[...].astype(F32)
    fresh_values = new_values[...].astype(F32)
    loads[4].wait()
    weights = []
    for r in range(own):
        spread = jnp.where(head_mask, asking[r : r + 1, :], 0.0)
        scores = dot_nt(spread.astype(BF16), cache_keys[r]) * factor
        own_score = jnp.sum(spread * fresh_keys[r : r + 1, :], axis=1, keepdims=True) * factor
        live = lax.broadcasted_iota(jnp.int32, (heads, cache), 1) < lengths[r]
        scores = jnp.where(live, scores, -1e30)
        highest = jnp.maximum(jnp.max(scores, axis=1, keepdims=True), own_score)
        cache_exp = jnp.where(live, jnp.exp(scores - highest), 0.0)
        own_exp = jnp.exp(own_score - highest)
        denom = jnp.sum(cache_exp, axis=1, keepdims=True) + own_exp
        weights.append(((cache_exp / denom).astype(BF16), (own_exp / denom).astype(BF16).astype(F32)))
    loads[5].wait()
    rows = []
    for r in range(own):
        cache_weight, own_weight = weights[r]
        full = dot(cache_weight, cache_values[r]) + own_weight * fresh_values[r : r + 1, :]
        rows.append(jnp.sum(jnp.where(head_mask, full, 0.0), axis=0, keepdims=True))
    attended = jnp.concatenate(rows, axis=0).astype(BF16).astype(F32)
    for d in range(n):
        start = d * share // LANES * LANES
        att_out[d] = attended[:, start : start + block]

    loads[6].wait()
    loads[7].wait()
    for slot in range(n // sections):
        picked = jnp.zeros((1, words), jnp.int32)
        for r in range(own):
            picked = picked + jnp.where(tile_slot[r] == slot, codes[r : r + 1, :], 0)
        slot_codes[slot] = picked

    pl.semaphore_wait(barrier, n - 1)

    @pl.loop(1, n)
    def _(k):
        att_copy(k).start()

    att_in[me] = att_out[me]

    @pl.loop(1, n)
    def _(k):
        code_copy(k).start()

    codes_in[me] = slot_codes[slot_of(me)]

    tile = lax.rem(me + sections // 2, n)
    section = lax.rem(tile, sections)
    tile_words = tile_h * IMG_W // 2
    span = (tile_h + 4) * IMG_W

    strip_words = -(-(span // 2) // LANES) * LANES
    place = lax.broadcasted_iota(jnp.int32, (span, strip_words), 0)
    word = lax.broadcasted_iota(jnp.int32, (span, strip_words), 1)
    gap = place - 2 * word
    even = jnp.where(gap == 0, 1.0, 0.0).astype(BF16)
    odd = jnp.where(gap == 1, 1.0, 0.0).astype(BF16)
    field[0:PAD, :] = jnp.zeros((PAD, 16), F32)
    field[PAD + span :, :] = jnp.zeros((PAD, 16), F32)
    loads[8].wait()
    whole = code_weight[...]
    top = whole.astype(BF16)
    rest = whole - top.astype(F32)
    middle = rest.astype(BF16)
    bottom = rest - middle.astype(F32)
    thirds = jnp.concatenate(
        [top.astype(F32), middle.astype(F32), bottom, jnp.zeros((1, channels), F32)], axis=0
    ).astype(BF16)

    @pl.loop(1, n)
    def _(k):
        att_copy(k).wait()

    for i in range(n):
        features[own * i : own * (i + 1), :] = att_in[i]
    rows_in = features[...].astype(BF16)
    loads[9].wait()
    pieces = part_out.shape[1] // own
    piece_width = width // pieces
    for c in range(pieces):
        piece = dot(rows_in, out_weight[:, c * piece_width : (c + 1) * piece_width])
        for j in range(piece_width // LANES):
            partial_rows[j, pl.ds(c, own * n, stride=pieces), :] = piece[
                :, j * LANES : (j + 1) * LANES
            ]
    for i in range(n):
        for j in range(piece_width // LANES):
            part_out[i, :, j * LANES : (j + 1) * LANES] = partial_rows[
                j, own * pieces * i : own * pieces * (i + 1), :
            ].astype(BF16)

    @pl.loop(1, n)
    def _(k):
        part_copy(k).start()

    part_in[me] = part_out[me]

    @pl.loop(1, n)
    def _(k):
        code_copy(k).wait()

    chosen = codes_in[0]
    for i in range(1, n):
        chosen = chosen + codes_in[i]
    turned = pltpu.roll(
        jnp.broadcast_to(chosen, (8, words)),
        lax.rem(words + IMG_W - section * tile_words, words),
        axis=1,
    )
    strip = turned[0:1, 0:strip_words]
    level = lax.broadcasted_iota(jnp.int32, (16, strip_words), 0)
    level = jnp.where(level >= 2 * FSQ_DIMS, level - 2 * FSQ_DIMS, level)
    level = jnp.where(level >= FSQ_DIMS, level - FSQ_DIMS, level)
    strip = jnp.broadcast_to(strip, (16, strip_words))

    def values_of(position_codes):
        levels = jnp.right_shift(position_codes, 3 * level) & 7
        return ((2 * levels - 7).astype(F32) * 0.125).astype(BF16)

    low = values_of(strip & 32767)
    high = values_of(jnp.right_shift(strip, 15))
    field[PAD : PAD + span, :] = dot_nt(even, low) + dot_nt(odd, high)


    def kept(count, rim):
        position = lax.broadcasted_iota(jnp.int32, (count, 1), 0)
        inside = jnp.logical_not(
            ((position < rim * IMG_W) & (section == 0))
            | ((position >= count - rim * IMG_W) & (section == sections - 1))
        )
        column = lax.rem(position, IMG_W)
        return inside, (column != 0, None, column != IMG_W - 1)

    inside, edges = kept(span, 2)
    for i in range(3):
        piece = field[PAD + i - 1 : PAD + i - 1 + span, :]
        mask = inside if edges[i] is None else inside & edges[i]
        piece = jnp.where(mask, piece, 0.0).astype(BF16)
        shifted[:, i * channels : (i + 1) * channels] = dot(piece, thirds).astype(BF16)

    mid_span = (tile_h + 2) * IMG_W
    loads[10].wait()
    hidden = dot(shifted[0:mid_span, :], conv_one[0])
    for tap in range(1, 3):
        hidden = hidden + dot(shifted[tap * IMG_W : tap * IMG_W + mid_span, :], conv_one[tap])
    inside, edges = kept(mid_span, 1)
    activated = jnp.where(inside, jax.nn.silu(hidden), 0.0)
    columns[0:PAD, :] = jnp.zeros((PAD, channels), F32)
    columns[PAD + mid_span :, :] = jnp.zeros((PAD, channels), F32)
    columns[PAD : PAD + mid_span, :] = activated

    for i in range(3):
        piece = columns[PAD + i - 1 : PAD + i - 1 + mid_span, :]
        if edges[i] is not None:
            piece = jnp.where(edges[i], piece, 0.0)
        shifted[0:mid_span, i * channels : (i + 1) * channels] = piece.astype(BF16)
    out_span = tile_h * IMG_W
    loads[11].wait()
    final = dot(shifted[0:out_span, :], conv_two[0])
    for tap in range(1, 3):
        final = final + dot(shifted[tap * IMG_W : tap * IMG_W + out_span, :], conv_two[tap])
    decoded[...] = final.astype(BF16)
    @pl.loop(1, n)
    def _(k):
        part_copy(k).wait()

    total = part_in[0].astype(F32)
    for i in range(1, n):
        total = total + part_in[i].astype(F32)
    mixed[...] = jnp.concatenate(
        [
            jnp.concatenate([total[r * pieces + c][None] for c in range(pieces)], axis=1)
            for r in range(own)
        ],
        axis=0,
    ).astype(BF16)


def on_device(
    n,
    queries,
    new_keys,
    new_values,
    cache_keys,
    cache_values,
    cache_lengths,
    out_weight,
    codes,
    tile_slot,
    code_weight,
    conv_one,
    conv_two,
):
    own, width = queries.shape
    channels = code_weight.shape[1]
    sections = IMG_SPLIT
    tile_h = IMG_H // sections
    share = out_weight.shape[0]
    block = max(share, LANES)
    if share < block:
        parts = block // share
        slot = lax.rem(lax.axis_index("rows"), parts)
        which = jnp.arange(parts, dtype=jnp.int32)[:, None, None] == slot
        out_weight = jnp.where(which, out_weight[None], jnp.zeros((), BF16)).reshape(block, width)
    taps = conv_one.shape[1] * channels
    conv_one = conv_one.reshape(3, taps, channels)
    conv_two = conv_two.reshape(3, taps, channels)
    pieces = 16 // own
    span = (tile_h + 4) * IMG_W
    mid_span = (tile_h + 2) * IMG_W
    out_span = tile_h * IMG_W
    vmem = pl.BlockSpec(memory_space=pltpu.VMEM)
    hbm = pl.BlockSpec(memory_space=pl.ANY)
    dma = pltpu.SemaphoreType.DMA
    mixed, decoded = pl.pallas_call(
        functools.partial(kernel, n, tile_h),
        out_shape=(
            pltpu.VMEM((own, width), BF16),
            pltpu.VMEM((out_span, channels), BF16),
        ),
        in_specs=[hbm] * 12,
        out_specs=(vmem, vmem),
        scratch_shapes=[
            pltpu.SMEM(cache_lengths.shape, jnp.int32),
            pltpu.SMEM(tile_slot.shape, jnp.int32),
            pltpu.VMEM(queries.shape, BF16),
            pltpu.VMEM(new_keys.shape, BF16),
            pltpu.VMEM(new_values.shape, BF16),
            pltpu.VMEM(codes.shape, jnp.int32),
            pltpu.VMEM(code_weight.shape, F32),
            pltpu.VMEM(cache_keys.shape, BF16),
            pltpu.VMEM(cache_values.shape, BF16),
            pltpu.VMEM(out_weight.shape, BF16),
            pltpu.VMEM(conv_one.shape, BF16),
            pltpu.VMEM(conv_two.shape, BF16),
            pltpu.VMEM((n // sections, 1, codes.shape[1]), jnp.int32),
            pltpu.VMEM((n, 1, codes.shape[1]), jnp.int32),
            pltpu.VMEM((n, own, block), F32),
            pltpu.VMEM((n, own, block), F32),
            pltpu.VMEM((n * own, block), F32),
            pltpu.VMEM((width // pieces // LANES, n * own * pieces, LANES), F32),
            pltpu.VMEM((n, own * pieces, width // pieces), BF16),
            pltpu.VMEM((n, own * pieces, width // pieces), BF16),
            pltpu.VMEM((span + 2 * PAD, 16), F32),
            pltpu.VMEM((mid_span + 2 * PAD, channels), F32),
            pltpu.VMEM((span, taps), BF16),
            dma((12,)),
            dma((n,)),
            dma((n,)),
            dma((n,)),
            dma((n,)),
            dma((n,)),
            dma((n,)),
        ],
        compiler_params=pltpu.CompilerParams(
            collective_id=0, has_side_effects=True, vmem_limit_bytes=60 * 1024 * 1024
        ),
        name="decode_step",
    )(
        cache_lengths,
        tile_slot,
        queries,
        new_keys,
        new_values,
        codes,
        code_weight,
        cache_keys,
        cache_values,
        out_weight,
        conv_one,
        conv_two,
    )
    return mixed, decoded.reshape(tile_h, IMG_W, channels)


def solution(mesh):
    both = ("groups", "rows")
    in_specs = (
        P(both, None),
        P(both, None),
        P(both, None),
        P(both, None, None),
        P(both, None, None),
        P(both),
        P("rows", None),
        P(both, None),
        P(both),
        P(),
        P(),
        P(),
    )
    out_specs = (P(both, None), P(both, None, None))
    return jax.shard_map(
        functools.partial(on_device, mesh.shape["rows"]),
        mesh=mesh,
        in_specs=in_specs,
        out_specs=out_specs,
        check_vma=False,
    )
```

```python
import functools
import math

import jax
import jax.numpy as jnp
from jax import lax
from jax.experimental import pallas as pl
from jax.experimental.pallas import tpu as pltpu
from jax.sharding import PartitionSpec as P

HEAD_DIM = 128
FSQ_DIMS = 5
IMG_H = 32
IMG_W = 48
IMG_SPLIT = 4
LANES = 128
PAD = 8
BF16 = jnp.bfloat16
F32 = jnp.float32
MESH = pl.DeviceIdType.MESH


def dot(a, b):
    return jnp.dot(a, b, preferred_element_type=F32)


def dot_nt(a, b):
    return lax.dot_general(a, b, (((1,), (1,)), ((), ())), preferred_element_type=F32)


def kernel(
    n,
    tile_h,
    lengths_hbm,
    tile_slot_hbm,
    queries_hbm,
    new_keys_hbm,
    new_values_hbm,
    codes_hbm,
    code_weight_hbm,
    cache_keys_hbm,
    cache_values_hbm,
    out_weight_hbm,
    conv_one_hbm,
    conv_two_hbm,
    mixed,
    decoded,
    lengths,
    tile_slot,
    queries,
    new_keys,
    new_values,
    codes,
    code_weight,
    cache_keys,
    cache_values,
    out_weight,
    conv_one,
    conv_two,
    slot_codes,
    codes_in,
    att_out,
    att_in,
    features,
    partial_rows,
    part_out,
    part_in,
    field,
    columns,
    shifted,
    local_sem,
    code_send,
    code_recv,
    att_send,
    att_recv,
    part_send,
    part_recv,
):
    me = lax.axis_index("rows")
    own = queries.shape[0]
    width = queries.shape[1]
    heads = width // HEAD_DIM
    cache = cache_keys.shape[1]
    channels = code_weight.shape[1]
    sections = IMG_H // tile_h
    share = width // n
    block = att_out.shape[2]
    words = codes.shape[1]
    tile_words = tile_h * IMG_W // 2
    span = (tile_h + 4) * IMG_W
    strip_words = slot_codes.shape[2]

    barrier = pltpu.get_barrier_semaphore()

    @pl.loop(1, n)
    def _(k):
        pl.semaphore_signal(
            barrier, inc=1, device_id={"rows": lax.rem(me + k, n)}, device_id_type=MESH
        )

    loads = [
        pltpu.make_async_copy(source, target, local_sem.at[i])
        for i, (source, target) in enumerate(
            (
                (queries_hbm, queries),
                (new_keys_hbm, new_keys),
                (new_values_hbm, new_values),
                (lengths_hbm, lengths),
                (cache_keys_hbm, cache_keys),
                (cache_values_hbm, cache_values),
                (codes_hbm, codes),
                (tile_slot_hbm, tile_slot),
                (code_weight_hbm, code_weight),
                (out_weight_hbm, out_weight),
                (conv_one_hbm, conv_one),
                (conv_two_hbm, conv_two),
            )
        )
    ]
    for load in loads:
        load.start()

    def tile_of(device):
        return lax.rem(device + sections // 2, n)

    def code_copy(k):
        target = lax.rem(me + k, n)
        return pltpu.make_async_remote_copy(
            src_ref=slot_codes.at[tile_of(target)],
            dst_ref=codes_in.at[me],
            send_sem=code_send.at[k],
            recv_sem=code_recv.at[k],
            device_id={"rows": target},
            device_id_type=MESH,
        )

    def att_copy(k):
        target = lax.rem(me + k, n)
        return pltpu.make_async_remote_copy(
            src_ref=att_out.at[target],
            dst_ref=att_in.at[me],
            send_sem=att_send.at[k],
            recv_sem=att_recv.at[k],
            device_id={"rows": target},
            device_id_type=MESH,
        )

    def part_copy(k):
        target = lax.rem(me + k, n)
        return pltpu.make_async_remote_copy(
            src_ref=part_out.at[target],
            dst_ref=part_in.at[me],
            send_sem=part_send.at[k],
            recv_sem=part_recv.at[k],
            device_id={"rows": target},
            device_id_type=MESH,
        )

    head_mask = (
        lax.broadcasted_iota(jnp.int32, (heads, width), 1) // HEAD_DIM
        == lax.broadcasted_iota(jnp.int32, (heads, width), 0)
    )
    factor = 1.0 / math.sqrt(HEAD_DIM)
    loads[0].wait()
    loads[1].wait()
    loads[2].wait()
    loads[3].wait()
    asking = queries[...].astype(F32)
    fresh_keys = new_keys[...].astype(F32)
    fresh_values = new_values[...].astype(F32)
    loads[4].wait()
    weights = []
    for r in range(own):
        spread = jnp.where(head_mask, asking[r : r + 1, :], 0.0)
        scores = dot_nt(spread.astype(BF16), cache_keys[r]) * factor
        own_score = jnp.sum(spread * fresh_keys[r : r + 1, :], axis=1, keepdims=True) * factor
        live = lax.broadcasted_iota(jnp.int32, (heads, cache), 1) < lengths[r]
        scores = jnp.where(live, scores, -1e30)
        highest = jnp.maximum(jnp.max(scores, axis=1, keepdims=True), own_score)
        cache_exp = jnp.where(live, jnp.exp(scores - highest), 0.0)
        own_exp = jnp.exp(own_score - highest)
        denom = jnp.sum(cache_exp, axis=1, keepdims=True) + own_exp
        weights.append(((cache_exp / denom).astype(BF16), (own_exp / denom).astype(BF16).astype(F32)))
    loads[5].wait()
    rows = []
    for r in range(own):
        cache_weight, own_weight = weights[r]
        full = dot(cache_weight, cache_values[r]) + own_weight * fresh_values[r : r + 1, :]
        rows.append(jnp.sum(jnp.where(head_mask, full, 0.0), axis=0, keepdims=True))
    attended = jnp.concatenate(rows, axis=0).astype(BF16)
    for d in range(n):
        start = d * share // LANES * LANES
        att_out[d] = attended[:, start : start + block]

    loads[6].wait()
    loads[7].wait()
    for slot in range(n // sections):
        picked = jnp.zeros((1, words), jnp.int32)
        for r in range(own):
            picked = picked + jnp.where(tile_slot[r] == slot, codes[r : r + 1, :], 0)
        picked = jnp.broadcast_to(picked, (8, words))
        for part in range(sections):
            shift = (IMG_W - part * tile_words) % words
            turned = pltpu.roll(picked, shift, axis=1) if shift else picked
            slot_codes[slot * sections + part] = turned[0:1, 0:strip_words]

    pl.semaphore_wait(barrier, n - 1)

    @pl.loop(1, n)
    def _(k):
        att_copy(k).start()

    att_in[me] = att_out[me]

    @pl.loop(1, n)
    def _(k):
        code_copy(k).start()

    codes_in[me] = slot_codes[tile_of(me)]

    tile = lax.rem(me + sections // 2, n)
    section = lax.rem(tile, sections)

    place = lax.broadcasted_iota(jnp.int32, (span, strip_words), 0)
    word = lax.broadcasted_iota(jnp.int32, (span, strip_words), 1)
    gap = place - 2 * word
    even = jnp.where(gap == 0, 1.0, 0.0).astype(BF16)
    odd = jnp.where(gap == 1, 1.0, 0.0).astype(BF16)
    field[0:PAD, :] = jnp.zeros((PAD, 16), F32)
    field[PAD + span :, :] = jnp.zeros((PAD, 16), F32)
    loads[8].wait()
    whole = code_weight[...]
    top = whole.astype(BF16)
    rest = whole - top.astype(F32)
    middle = rest.astype(BF16)
    bottom = rest - middle.astype(F32)
    thirds = jnp.concatenate(
        [top.astype(F32), middle.astype(F32), bottom, jnp.zeros((1, channels), F32)], axis=0
    ).astype(BF16)

    @pl.loop(1, n)
    def _(k):
        att_copy(k).wait()

    for i in range(n):
        features[own * i : own * (i + 1), :] = att_in[i].astype(F32)
    rows_in = features[...].astype(BF16)
    loads[9].wait()
    pieces = part_out.shape[1] // own
    piece_width = width // pieces
    for c in range(pieces):
        piece = dot(rows_in, out_weight[:, c * piece_width : (c + 1) * piece_width])
        for j in range(piece_width // LANES):
            partial_rows[j, pl.ds(c, own * n, stride=pieces), :] = piece[
                :, j * LANES : (j + 1) * LANES
            ]
    for i in range(n):
        for j in range(piece_width // LANES):
            part_out[i, :, j * LANES : (j + 1) * LANES] = partial_rows[
                j, own * pieces * i : own * pieces * (i + 1), :
            ].astype(BF16)

    @pl.loop(1, n)
    def _(k):
        part_copy(k).start()

    part_in[me] = part_out[me]

    @pl.loop(1, n)
    def _(k):
        code_copy(k).wait()

    chosen = codes_in[0]
    for i in range(1, n):
        chosen = chosen + codes_in[i]
    level = lax.broadcasted_iota(jnp.int32, (16, strip_words), 0)
    level = jnp.where(level >= 2 * FSQ_DIMS, level - 2 * FSQ_DIMS, level)
    level = jnp.where(level >= FSQ_DIMS, level - FSQ_DIMS, level)
    strip = jnp.broadcast_to(chosen, (16, strip_words))

    def values_of(position_codes):
        levels = jnp.right_shift(position_codes, 3 * level) & 7
        return ((2 * levels - 7).astype(F32) * 0.125).astype(BF16)

    low = values_of(strip & 32767)
    high = values_of(jnp.right_shift(strip, 15))
    field[PAD : PAD + span, :] = dot_nt(even, low) + dot_nt(odd, high)


    def kept(count, rim):
        position = lax.broadcasted_iota(jnp.int32, (count, 1), 0)
        inside = jnp.logical_not(
            ((position < rim * IMG_W) & (section == 0))
            | ((position >= count - rim * IMG_W) & (section == sections - 1))
        )
        column = lax.rem(position, IMG_W)
        return inside, (column != 0, None, column != IMG_W - 1)

    inside, edges = kept(span, 2)
    for i in range(3):
        piece = field[PAD + i - 1 : PAD + i - 1 + span, :]
        mask = inside if edges[i] is None else inside & edges[i]
        piece = jnp.where(mask, piece, 0.0).astype(BF16)
        shifted[:, i * channels : (i + 1) * channels] = dot(piece, thirds).astype(BF16)

    mid_span = (tile_h + 2) * IMG_W
    loads[10].wait()
    hidden = dot(shifted[0:mid_span, :], conv_one[0])
    for tap in range(1, 3):
        hidden = hidden + dot(shifted[tap * IMG_W : tap * IMG_W + mid_span, :], conv_one[tap])
    inside, edges = kept(mid_span, 1)
    activated = jnp.where(inside, jax.nn.silu(hidden), 0.0)
    columns[0:PAD, :] = jnp.zeros((PAD, channels), F32)
    columns[PAD + mid_span :, :] = jnp.zeros((PAD, channels), F32)
    columns[PAD : PAD + mid_span, :] = activated

    for i in range(3):
        piece = columns[PAD + i - 1 : PAD + i - 1 + mid_span, :]
        if edges[i] is not None:
            piece = jnp.where(edges[i], piece, 0.0)
        shifted[0:mid_span, i * channels : (i + 1) * channels] = piece.astype(BF16)
    out_span = tile_h * IMG_W
    loads[11].wait()
    final = dot(shifted[0:out_span, :], conv_two[0])
    for tap in range(1, 3):
        final = final + dot(shifted[tap * IMG_W : tap * IMG_W + out_span, :], conv_two[tap])
    decoded[...] = final.astype(BF16)
    @pl.loop(1, n)
    def _(k):
        part_copy(k).wait()

    total = part_in[0].astype(F32)
    for i in range(1, n):
        total = total + part_in[i].astype(F32)
    mixed[...] = jnp.concatenate(
        [
            jnp.concatenate([total[r * pieces + c][None] for c in range(pieces)], axis=1)
            for r in range(own)
        ],
        axis=0,
    ).astype(BF16)


def settle_kernel(mixed, decoded, mixed_out, decoded_out, sems):
    stores = [
        pltpu.make_async_copy(decoded, decoded_out, sems.at[0]),
        pltpu.make_async_copy(mixed, mixed_out, sems.at[1]),
    ]
    for store in stores:
        store.start()
    for store in stores:
        store.wait()


def settle(mixed, decoded):
    hbm = pl.BlockSpec(memory_space=pltpu.HBM)
    vmem = pl.BlockSpec(memory_space=pltpu.VMEM)
    return pl.pallas_call(
        settle_kernel,
        out_shape=(
            jax.ShapeDtypeStruct(mixed.shape, mixed.dtype),
            jax.ShapeDtypeStruct(decoded.shape, decoded.dtype),
        ),
        in_specs=[vmem, vmem],
        out_specs=(hbm, hbm),
        scratch_shapes=[pltpu.SemaphoreType.DMA((2,))],
        compiler_params=pltpu.CompilerParams(vmem_limit_bytes=2 * 1024 * 1024),
        name="settle",
    )(mixed, decoded)


def on_device(
    n,
    queries,
    new_keys,
    new_values,
    cache_keys,
    cache_values,
    cache_lengths,
    out_weight,
    codes,
    tile_slot,
    code_weight,
    conv_one,
    conv_two,
):
    own, width = queries.shape
    channels = code_weight.shape[1]
    sections = IMG_SPLIT
    tile_h = IMG_H // sections
    share = out_weight.shape[0]
    block = max(share, LANES)
    if share < block:
        parts = block // share
        slot = lax.rem(lax.axis_index("rows"), parts)
        which = jnp.arange(parts, dtype=jnp.int32)[:, None, None] == slot
        out_weight = jnp.where(which, out_weight[None], jnp.zeros((), BF16)).reshape(block, width)
    taps = conv_one.shape[1] * channels
    conv_one = conv_one.reshape(3, taps, channels)
    conv_two = conv_two.reshape(3, taps, channels)
    pieces = 16 // own
    span = (tile_h + 4) * IMG_W
    strip_words = -(-(span // 2) // LANES) * LANES
    mid_span = (tile_h + 2) * IMG_W
    out_span = tile_h * IMG_W
    vmem = pl.BlockSpec(memory_space=pltpu.VMEM)
    hbm = pl.BlockSpec(memory_space=pl.ANY)
    dma = pltpu.SemaphoreType.DMA
    mixed, decoded = pl.pallas_call(
        functools.partial(kernel, n, tile_h),
        out_shape=(
            pltpu.VMEM((own, width), BF16),
            pltpu.VMEM((out_span, channels), BF16),
        ),
        in_specs=[hbm] * 12,
        out_specs=(vmem, vmem),
        scratch_shapes=[
            pltpu.SMEM(cache_lengths.shape, jnp.int32),
            pltpu.SMEM(tile_slot.shape, jnp.int32),
            pltpu.VMEM(queries.shape, BF16),
            pltpu.VMEM(new_keys.shape, BF16),
            pltpu.VMEM(new_values.shape, BF16),
            pltpu.VMEM(codes.shape, jnp.int32),
            pltpu.VMEM(code_weight.shape, F32),
            pltpu.VMEM(cache_keys.shape, BF16),
            pltpu.VMEM(cache_values.shape, BF16),
            pltpu.VMEM(out_weight.shape, BF16),
            pltpu.VMEM(conv_one.shape, BF16),
            pltpu.VMEM(conv_two.shape, BF16),
            pltpu.VMEM((n, 1, strip_words), jnp.int32),
            pltpu.VMEM((n, 1, strip_words), jnp.int32),
            pltpu.VMEM((n, own, block), BF16),
            pltpu.VMEM((n, own, block), BF16),
            pltpu.VMEM((n * own, block), F32),
            pltpu.VMEM((width // pieces // LANES, n * own * pieces, LANES), F32),
            pltpu.VMEM((n, own * pieces, width // pieces), BF16),
            pltpu.VMEM((n, own * pieces, width // pieces), BF16),
            pltpu.VMEM((span + 2 * PAD, 16), F32),
            pltpu.VMEM((mid_span + 2 * PAD, channels), F32),
            pltpu.VMEM((span, taps), BF16),
            dma((12,)),
            dma((n,)),
            dma((n,)),
            dma((n,)),
            dma((n,)),
            dma((n,)),
            dma((n,)),
        ],
        compiler_params=pltpu.CompilerParams(
            collective_id=0, has_side_effects=True, vmem_limit_bytes=60 * 1024 * 1024
        ),
        name="decode_step",
    )(
        cache_lengths,
        tile_slot,
        queries,
        new_keys,
        new_values,
        codes,
        code_weight,
        cache_keys,
        cache_values,
        out_weight,
        conv_one,
        conv_two,
    )
    mixed, decoded = settle(mixed, decoded)
    return mixed, decoded.reshape(tile_h, IMG_W, channels)


def solution(mesh):
    both = ("groups", "rows")
    in_specs = (
        P(both, None),
        P(both, None),
        P(both, None),
        P(both, None, None),
        P(both, None, None),
        P(both),
        P("rows", None),
        P(both, None),
        P(both),
        P(),
        P(),
        P(),
    )
    out_specs = (P(both, None), P(both, None, None))
    return jax.shard_map(
        functools.partial(on_device, mesh.shape["rows"]),
        mesh=mesh,
        in_specs=in_specs,
        out_specs=out_specs,
        check_vma=False,
    )
```

```python
import functools
import math

import jax
import jax.numpy as jnp
from jax import lax
from jax.experimental import pallas as pl
from jax.experimental.pallas import tpu as pltpu
from jax.sharding import PartitionSpec as P

HEAD_DIM = 128
FSQ_DIMS = 5
IMG_H = 32
IMG_W = 48
IMG_SPLIT = 4
LANES = 128
PAD = 8
BF16 = jnp.bfloat16
F32 = jnp.float32
MESH = pl.DeviceIdType.MESH


def dot(a, b):
    return jnp.dot(a, b, preferred_element_type=F32)


def dot_nt(a, b):
    return lax.dot_general(a, b, (((1,), (1,)), ((), ())), preferred_element_type=F32)


def kernel(
    n,
    tile_h,
    lengths_hbm,
    tile_slot_hbm,
    queries_hbm,
    new_keys_hbm,
    new_values_hbm,
    codes_hbm,
    code_weight_hbm,
    cache_keys_hbm,
    cache_values_hbm,
    out_weight_hbm,
    conv_one_hbm,
    conv_two_hbm,
    mixed,
    decoded,
    lengths,
    tile_slot,
    queries,
    new_keys,
    new_values,
    codes,
    code_weight,
    cache_keys,
    cache_values,
    out_weight,
    conv_one,
    conv_two,
    slot_codes,
    codes_in,
    att_out,
    att_in,
    features,
    partial_rows,
    part_out,
    part_in,
    field,
    fields,
    folds,
    columns,
    shifted,
    local_sem,
    code_send,
    code_recv,
    att_send,
    att_recv,
    part_send,
    part_recv,
):
    me = lax.axis_index("rows")
    own = queries.shape[0]
    width = queries.shape[1]
    heads = width // HEAD_DIM
    cache = cache_keys.shape[1]
    channels = code_weight.shape[1]
    sections = IMG_H // tile_h
    share = width // n
    block = att_out.shape[2]
    words = codes.shape[1]
    tile_words = tile_h * IMG_W // 2
    span = (tile_h + 4) * IMG_W
    strip_words = slot_codes.shape[2]

    barrier = pltpu.get_barrier_semaphore()

    @pl.loop(1, n)
    def _(k):
        pl.semaphore_signal(
            barrier, inc=1, device_id={"rows": lax.rem(me + k, n)}, device_id_type=MESH
        )

    loads = [
        pltpu.make_async_copy(source, target, local_sem.at[i])
        for i, (source, target) in enumerate(
            (
                (queries_hbm, queries),
                (new_keys_hbm, new_keys),
                (new_values_hbm, new_values),
                (lengths_hbm, lengths),
                (cache_keys_hbm, cache_keys),
                (cache_values_hbm, cache_values),
                (codes_hbm, codes),
                (tile_slot_hbm, tile_slot),
                (code_weight_hbm, code_weight),
                (out_weight_hbm, out_weight),
                (conv_one_hbm, conv_one),
                (conv_two_hbm, conv_two),
            )
        )
    ]
    for load in loads:
        load.start()

    def tile_of(device):
        return lax.rem(device + sections // 2, n)

    def code_copy(k):
        target = lax.rem(me + k, n)
        return pltpu.make_async_remote_copy(
            src_ref=slot_codes.at[tile_of(target)],
            dst_ref=codes_in.at[me],
            send_sem=code_send.at[k],
            recv_sem=code_recv.at[k],
            device_id={"rows": target},
            device_id_type=MESH,
        )

    def att_copy(k):
        target = lax.rem(me + k, n)
        return pltpu.make_async_remote_copy(
            src_ref=att_out.at[target],
            dst_ref=att_in.at[me],
            send_sem=att_send.at[k],
            recv_sem=att_recv.at[k],
            device_id={"rows": target},
            device_id_type=MESH,
        )

    def part_copy(k):
        target = lax.rem(me + k, n)
        return pltpu.make_async_remote_copy(
            src_ref=part_out.at[target],
            dst_ref=part_in.at[me],
            send_sem=part_send.at[k],
            recv_sem=part_recv.at[k],
            device_id={"rows": target},
            device_id_type=MESH,
        )

    head_mask = (
        lax.broadcasted_iota(jnp.int32, (heads, width), 1) // HEAD_DIM
        == lax.broadcasted_iota(jnp.int32, (heads, width), 0)
    )
    factor = 1.0 / math.sqrt(HEAD_DIM)
    loads[0].wait()
    loads[1].wait()
    loads[2].wait()
    loads[3].wait()
    asking = queries[...].astype(F32)
    fresh_keys = new_keys[...].astype(F32)
    fresh_values = new_values[...].astype(F32)
    loads[4].wait()
    weights = []
    for r in range(own):
        spread = jnp.where(head_mask, asking[r : r + 1, :], 0.0)
        scores = dot_nt(spread.astype(BF16), cache_keys[r]) * factor
        own_score = jnp.sum(spread * fresh_keys[r : r + 1, :], axis=1, keepdims=True) * factor
        live = lax.broadcasted_iota(jnp.int32, (heads, cache), 1) < lengths[r]
        scores = jnp.where(live, scores, -1e30)
        highest = jnp.maximum(jnp.max(scores, axis=1, keepdims=True), own_score)
        cache_exp = jnp.where(live, jnp.exp(scores - highest), 0.0)
        own_exp = jnp.exp(own_score - highest)
        denom = jnp.sum(cache_exp, axis=1, keepdims=True) + own_exp
        weights.append(((cache_exp / denom).astype(BF16), (own_exp / denom).astype(BF16).astype(F32)))
    loads[5].wait()
    rows = []
    for r in range(own):
        cache_weight, own_weight = weights[r]
        full = dot(cache_weight, cache_values[r]) + own_weight * fresh_values[r : r + 1, :]
        rows.append(jnp.sum(jnp.where(head_mask, full, 0.0), axis=0, keepdims=True))
    attended = jnp.concatenate(rows, axis=0).astype(BF16)
    for d in range(n):
        start = d * share // LANES * LANES
        att_out[d] = attended[:, start : start + block]

    loads[6].wait()
    loads[7].wait()
    for slot in range(n // sections):
        picked = jnp.zeros((1, words), jnp.int32)
        for r in range(own):
            picked = picked + jnp.where(tile_slot[r] == slot, codes[r : r + 1, :], 0)
        picked = jnp.broadcast_to(picked, (8, words))
        for part in range(sections):
            shift = (IMG_W - part * tile_words) % words
            turned = pltpu.roll(picked, shift, axis=1) if shift else picked
            slot_codes[slot * sections + part] = turned[0:1, 0:strip_words]

    pl.semaphore_wait(barrier, n - 1)

    @pl.loop(1, n)
    def _(k):
        att_copy(k).start()

    att_in[me] = att_out[me]

    @pl.loop(1, n)
    def _(k):
        code_copy(k).start()

    codes_in[me] = slot_codes[tile_of(me)]

    tile = lax.rem(me + sections // 2, n)
    section = lax.rem(tile, sections)

    place = lax.broadcasted_iota(jnp.int32, (span, strip_words), 0)
    word = lax.broadcasted_iota(jnp.int32, (span, strip_words), 1)
    gap = place - 2 * word
    even = jnp.where(gap == 0, 1.0, 0.0).astype(BF16)
    odd = jnp.where(gap == 1, 1.0, 0.0).astype(BF16)
    field[0:PAD, :] = jnp.zeros((PAD, 16), F32)
    field[PAD + span :, :] = jnp.zeros((PAD, 16), F32)
    loads[8].wait()
    whole = code_weight[...]
    top = whole.astype(BF16)
    rest = whole - top.astype(F32)
    middle = rest.astype(BF16)
    bottom = rest - middle.astype(F32)
    thirds = jnp.concatenate(
        [top.astype(F32), middle.astype(F32), bottom, jnp.zeros((1, channels), F32)], axis=0
    ).astype(BF16)

    loads[10].wait()
    for tap in range(3):
        for i in range(3):
            wide = dot(thirds, conv_one[tap, i * channels : (i + 1) * channels, :])
            folded = (
                wide[0:FSQ_DIMS]
                + wide[FSQ_DIMS : 2 * FSQ_DIMS]
                + wide[2 * FSQ_DIMS : 3 * FSQ_DIMS]
            )
            head = folded.astype(BF16).astype(F32)
            body = (folded - head).astype(BF16).astype(F32)
            tail = folded - head - body
            folds[tap, 16 * i : 16 * (i + 1), :] = jnp.concatenate(
                [head, body, tail, jnp.zeros((1, channels), F32)], axis=0
            ).astype(BF16)

    @pl.loop(1, n)
    def _(k):
        att_copy(k).wait()

    for i in range(n):
        features[own * i : own * (i + 1), :] = att_in[i].astype(F32)
    rows_in = features[...].astype(BF16)
    loads[9].wait()
    pieces = part_out.shape[1] // own
    piece_width = width // pieces
    for c in range(pieces):
        piece = dot(rows_in, out_weight[:, c * piece_width : (c + 1) * piece_width])
        for j in range(piece_width // LANES):
            partial_rows[j, pl.ds(c, own * n, stride=pieces), :] = piece[
                :, j * LANES : (j + 1) * LANES
            ]
    for i in range(n):
        for j in range(piece_width // LANES):
            part_out[i, :, j * LANES : (j + 1) * LANES] = partial_rows[
                j, own * pieces * i : own * pieces * (i + 1), :
            ].astype(BF16)

    @pl.loop(1, n)
    def _(k):
        part_copy(k).start()

    part_in[me] = part_out[me]

    @pl.loop(1, n)
    def _(k):
        code_copy(k).wait()

    chosen = codes_in[0]
    for i in range(1, n):
        chosen = chosen + codes_in[i]
    level = lax.broadcasted_iota(jnp.int32, (16, strip_words), 0)
    level = jnp.where(level >= 2 * FSQ_DIMS, level - 2 * FSQ_DIMS, level)
    level = jnp.where(level >= FSQ_DIMS, level - FSQ_DIMS, level)
    strip = jnp.broadcast_to(chosen, (16, strip_words))

    def values_of(position_codes):
        levels = jnp.right_shift(position_codes, 3 * level) & 7
        return ((2 * levels - 7).astype(F32) * 0.125).astype(BF16)

    low = values_of(strip & 32767)
    high = values_of(jnp.right_shift(strip, 15))
    field[PAD : PAD + span, :] = dot_nt(even, low) + dot_nt(odd, high)


    def kept(count, rim):
        position = lax.broadcasted_iota(jnp.int32, (count, 1), 0)
        inside = jnp.logical_not(
            ((position < rim * IMG_W) & (section == 0))
            | ((position >= count - rim * IMG_W) & (section == sections - 1))
        )
        column = lax.rem(position, IMG_W)
        return inside, (column != 0, None, column != IMG_W - 1)

    inside, edges = kept(span, 2)
    for i in range(3):
        piece = field[PAD + i - 1 : PAD + i - 1 + span, :]
        mask = inside if edges[i] is None else inside & edges[i]
        fields[:, 16 * i : 16 * (i + 1)] = jnp.where(mask, piece, 0.0)

    mid_span = (tile_h + 2) * IMG_W
    hidden = dot(fields[0:mid_span, :].astype(BF16), folds[0])
    for tap in range(1, 3):
        hidden = hidden + dot(
            fields[tap * IMG_W : tap * IMG_W + mid_span, :].astype(BF16), folds[tap]
        )
    inside, edges = kept(mid_span, 1)
    activated = jnp.where(inside, jax.nn.silu(hidden), 0.0)
    columns[0:PAD, :] = jnp.zeros((PAD, channels), F32)
    columns[PAD + mid_span :, :] = jnp.zeros((PAD, channels), F32)
    columns[PAD : PAD + mid_span, :] = activated

    for i in range(3):
        piece = columns[PAD + i - 1 : PAD + i - 1 + mid_span, :]
        if edges[i] is not None:
            piece = jnp.where(edges[i], piece, 0.0)
        shifted[0:mid_span, i * channels : (i + 1) * channels] = piece.astype(BF16)
    out_span = tile_h * IMG_W
    loads[11].wait()
    final = dot(shifted[0:out_span, :], conv_two[0])
    for tap in range(1, 3):
        final = final + dot(shifted[tap * IMG_W : tap * IMG_W + out_span, :], conv_two[tap])
    decoded[...] = final.astype(BF16)
    @pl.loop(1, n)
    def _(k):
        part_copy(k).wait()

    total = part_in[0].astype(F32)
    for i in range(1, n):
        total = total + part_in[i].astype(F32)
    mixed[...] = jnp.concatenate(
        [
            jnp.concatenate([total[r * pieces + c][None] for c in range(pieces)], axis=1)
            for r in range(own)
        ],
        axis=0,
    ).astype(BF16)


def settle_kernel(mixed, decoded, mixed_out, decoded_out, sems):
    stores = [
        pltpu.make_async_copy(decoded, decoded_out, sems.at[0]),
        pltpu.make_async_copy(mixed, mixed_out, sems.at[1]),
    ]
    for store in stores:
        store.start()
    for store in stores:
        store.wait()


def settle(mixed, decoded):
    hbm = pl.BlockSpec(memory_space=pltpu.HBM)
    vmem = pl.BlockSpec(memory_space=pltpu.VMEM)
    return pl.pallas_call(
        settle_kernel,
        out_shape=(
            jax.ShapeDtypeStruct(mixed.shape, mixed.dtype),
            jax.ShapeDtypeStruct(decoded.shape, decoded.dtype),
        ),
        in_specs=[vmem, vmem],
        out_specs=(hbm, hbm),
        scratch_shapes=[pltpu.SemaphoreType.DMA((2,))],
        compiler_params=pltpu.CompilerParams(vmem_limit_bytes=2 * 1024 * 1024),
        name="settle",
    )(mixed, decoded)


def on_device(
    n,
    queries,
    new_keys,
    new_values,
    cache_keys,
    cache_values,
    cache_lengths,
    out_weight,
    codes,
    tile_slot,
    code_weight,
    conv_one,
    conv_two,
):
    own, width = queries.shape
    channels = code_weight.shape[1]
    sections = IMG_SPLIT
    tile_h = IMG_H // sections
    share = out_weight.shape[0]
    block = max(share, LANES)
    if share < block:
        parts = block // share
        slot = lax.rem(lax.axis_index("rows"), parts)
        which = jnp.arange(parts, dtype=jnp.int32)[:, None, None] == slot
        out_weight = jnp.where(which, out_weight[None], jnp.zeros((), BF16)).reshape(block, width)
    taps = conv_one.shape[1] * channels
    conv_one = conv_one.reshape(3, taps, channels)
    conv_two = conv_two.reshape(3, taps, channels)
    pieces = 16 // own
    span = (tile_h + 4) * IMG_W
    strip_words = -(-(span // 2) // LANES) * LANES
    mid_span = (tile_h + 2) * IMG_W
    out_span = tile_h * IMG_W
    vmem = pl.BlockSpec(memory_space=pltpu.VMEM)
    hbm = pl.BlockSpec(memory_space=pl.ANY)
    dma = pltpu.SemaphoreType.DMA
    mixed, decoded = pl.pallas_call(
        functools.partial(kernel, n, tile_h),
        out_shape=(
            pltpu.VMEM((own, width), BF16),
            pltpu.VMEM((out_span, channels), BF16),
        ),
        in_specs=[hbm] * 12,
        out_specs=(vmem, vmem),
        scratch_shapes=[
            pltpu.SMEM(cache_lengths.shape, jnp.int32),
            pltpu.SMEM(tile_slot.shape, jnp.int32),
            pltpu.VMEM(queries.shape, BF16),
            pltpu.VMEM(new_keys.shape, BF16),
            pltpu.VMEM(new_values.shape, BF16),
            pltpu.VMEM(codes.shape, jnp.int32),
            pltpu.VMEM(code_weight.shape, F32),
            pltpu.VMEM(cache_keys.shape, BF16),
            pltpu.VMEM(cache_values.shape, BF16),
            pltpu.VMEM(out_weight.shape, BF16),
            pltpu.VMEM(conv_one.shape, BF16),
            pltpu.VMEM(conv_two.shape, BF16),
            pltpu.VMEM((n, 1, strip_words), jnp.int32),
            pltpu.VMEM((n, 1, strip_words), jnp.int32),
            pltpu.VMEM((n, own, block), BF16),
            pltpu.VMEM((n, own, block), BF16),
            pltpu.VMEM((n * own, block), F32),
            pltpu.VMEM((width // pieces // LANES, n * own * pieces, LANES), F32),
            pltpu.VMEM((n, own * pieces, width // pieces), BF16),
            pltpu.VMEM((n, own * pieces, width // pieces), BF16),
            pltpu.VMEM((span + 2 * PAD, 16), F32),
            pltpu.VMEM((span, 48), F32),
            pltpu.VMEM((3, 48, channels), BF16),
            pltpu.VMEM((mid_span + 2 * PAD, channels), F32),
            pltpu.VMEM((mid_span, taps), BF16),
            dma((12,)),
            dma((n,)),
            dma((n,)),
            dma((n,)),
            dma((n,)),
            dma((n,)),
            dma((n,)),
        ],
        compiler_params=pltpu.CompilerParams(
            collective_id=0, has_side_effects=True, vmem_limit_bytes=60 * 1024 * 1024
        ),
        name="decode_step",
    )(
        cache_lengths,
        tile_slot,
        queries,
        new_keys,
        new_values,
        codes,
        code_weight,
        cache_keys,
        cache_values,
        out_weight,
        conv_one,
        conv_two,
    )
    mixed, decoded = settle(mixed, decoded)
    return mixed, decoded.reshape(tile_h, IMG_W, channels)


def solution(mesh):
    both = ("groups", "rows")
    in_specs = (
        P(both, None),
        P(both, None),
        P(both, None),
        P(both, None, None),
        P(both, None, None),
        P(both),
        P("rows", None),
        P(both, None),
        P(both),
        P(),
        P(),
        P(),
    )
    out_specs = (P(both, None), P(both, None, None))
    return jax.shard_map(
        functools.partial(on_device, mesh.shape["rows"]),
        mesh=mesh,
        in_specs=in_specs,
        out_specs=out_specs,
        check_vma=False,
    )
```
